128 devices in a mesh: aux: 64 (over z, y, x), bas: 2 (over core).
Axes of the slice: x: 4, y: 4, z: 4, core: 2. Of those that a mesh axis runs over, the one named last changes fastest.
Arguments:
- integrals: bfloat16 [64, 128, 3, 128, 128], P('aux', 'bas'), may hold values from -0.0625 to 0.0625
- orbitals: bfloat16 [128, 128, 128], P('bas'), may hold values from -0.5 to 0.5
- locality: int32 [128], P('bas'), may hold values from 0 to 63, as said below
- screen: int32 [64, 128, 3], P('aux', 'bas'), may hold values 0 or 1
- metric: bfloat16 [64, 64], replicated, may hold values from -1 to 3
Outputs:
- exchange_band: float32 [128, 5, 16384], P('bas', None, 'aux')
The draws below stay inside these ranges and needn't reach their ends.
Inputs may be any that keep to these rules, and one draw needn't show every extreme that they name: `locality`: within each bas shard, its 64 orbital tiles name each of its 64 blocks exactly once.
All inputs are finite; a program needn't handle non-finite values. No bound on the sum of `screen` on one device may be relied on, other than what follows from the above.
Results may differ from the reference program's by a relative error of at most 0.00096.
Values may be sent and summed in bfloat16 or wider, within the bound.
A program may use at most 128 MiB of HBM per device.

```python
import jax
import jax.numpy as jnp
from jax import lax

TILE = 128
W = 3
AUX_DEV = 1
OPD = 1
NAUX = 64
AUX_TILES = 64
BLK_DEV = 64
NBLK = 128
NORBT = 128
N_AUX = 64


def draw_metric(key, part):
    key_off, key_diag = jax.random.split(key)
    spread = 0.5
    upper_end = 2.0
    noise_part = jnp.clip(jax.random.normal(key_off, (NAUX, NAUX), jnp.float32), -4.0, 4.0) * (spread / NAUX ** 0.5)
    diag_values = jax.random.uniform(key_diag, (NAUX,), jnp.float32, 1.0, upper_end)
    on_diagonal = jnp.arange(NAUX)[:, None] == jnp.arange(NAUX)[None, :]
    return jnp.where(on_diagonal, diag_values[:, None], noise_part).astype(jnp.bfloat16)


def draw_locality(key, part):
    shard_keys = jax.random.split(jax.random.fold_in(key, 17), NBLK // BLK_DEV)
    orders = jax.vmap(lambda one_key: jax.random.permutation(one_key, BLK_DEV))(shard_keys)
    return orders.reshape(-1).astype(jnp.int32)


def place_ends(entries, rng, low, largest):
    spot = [jax.random.randint(jax.random.fold_in(rng, axis), (), 0, length) for axis, length in enumerate(entries.shape)]
    main_axis = entries.shape.index(max(entries.shape))
    beside = spot[:main_axis] + [(spot[main_axis] + 1) % entries.shape[main_axis]] + spot[main_axis + 1:]
    return entries.at[tuple(spot)].set(low).at[tuple(beside)].set(largest)


def level_of(rng, shape, pieces, smallest, top_value):
    level, own = 1.0, jax.random.fold_in(rng, 6)
    for dim, parts in pieces:
        steps = jnp.exp(jax.random.uniform(jax.random.fold_in(own, dim), (parts,), jnp.float32, smallest / len(pieces), top_value / len(pieces)))
        level = level * jnp.repeat(steps, shape[dim] // parts).reshape([-1 if axis == dim else 1 for axis in range(len(shape))])
    return level


def centred(rng, extent, scale, bound, cuts=(), held_as=jnp.bfloat16):
    array = scale * jax.random.normal(rng, extent, jnp.float32)
    if cuts:
        array = array * level_of(rng, extent, cuts, -0.22, 0.18)
    return jnp.clip(array, -bound, bound).astype(held_as)


def setup_inputs(seed: int = 0) -> dict:
    keys = jax.random.split(jax.random.key(seed), 6)
    integrals = centred(keys[0], (NAUX, NBLK, W, TILE, TILE), (1.0 / (720 * NAUX) ** 0.5), 0.0625, ((0, 64), (1, 2)))
    orbitals = centred(keys[1], (NORBT, TILE, TILE), TILE ** -0.5, 0.5, ((0, 2),))
    locality = draw_locality(jax.random.fold_in(keys[5], 71), 0)
    screen = place_ends((jax.random.randint(keys[3], (AUX_TILES, NORBT, W), 0, 4) < 3).astype(jnp.int32), jax.random.fold_in(keys[3], 1), 0, 1)
    metric = draw_metric(jax.random.fold_in(keys[5], 71), 0)
    return {"integrals": integrals, "orbitals": orbitals, "locality": locality, "screen": screen, "metric": metric}


def reference(integrals, orbitals, locality, screen, metric):
    aux_count, block_count, reach_width, tile_size, _ = integrals.shape
    reach_blocks = reach_width // 2
    orbital_count = orbitals.shape[0]
    tile_ids = jnp.arange(orbital_count, dtype=jnp.int32)
    centres = ((tile_ids // (OPD * N_AUX)) * BLK_DEV + locality).astype(jnp.int32)
    aux_tiles = (jnp.arange(aux_count, dtype=jnp.int32) // AUX_DEV).astype(jnp.int32)
    offsets = jnp.arange(reach_width, dtype=jnp.int32)
    band_shape = (block_count + 2 * reach_blocks, 2 * reach_width - 1, tile_size, tile_size)

    def one_tile(band_sum, inputs):
        coefficients, centre_block, flag_rows = inputs
        chosen = lax.dynamic_index_in_dim(integrals, centre_block, axis=1, keepdims=False)
        half_rows = jnp.dot(chosen.reshape(-1, tile_size), coefficients, preferred_element_type=jnp.float32)
        half_rows = half_rows.reshape(aux_count, reach_width, tile_size, tile_size)
        row_blocks = centre_block + offsets - reach_blocks
        inside = ((row_blocks >= 0) & (row_blocks < block_count)).astype(jnp.float32)
        keep_mask = jnp.take(flag_rows, aux_tiles, axis=0).astype(jnp.float32) * inside[None, :]
        half_rows = (half_rows * keep_mask[:, :, None, None]).astype(jnp.bfloat16)
        mixed_rows = jnp.dot(metric, half_rows.reshape(aux_count, -1), preferred_element_type=jnp.float32)
        mixed_rows = mixed_rows.astype(jnp.bfloat16).reshape(half_rows.shape).astype(jnp.float32)
        gram_block = lax.dot_general(mixed_rows, mixed_rows, (((0, 3), (0, 3)), ((), ())))
        for offset in range(reach_width):
            band_piece = jnp.transpose(gram_block[offset], (1, 0, 2))
            band_piece = jnp.pad(band_piece, ((reach_width - 1 - offset, offset), (0, 0), (0, 0)))
            band_sum = band_sum.at[centre_block + offset].add(band_piece)
        return band_sum, None

    band_sum, _ = lax.scan(one_tile, jnp.zeros(band_shape, jnp.float32), (orbitals, centres, jnp.transpose(screen, (1, 0, 2))))
    result = band_sum[reach_blocks:reach_blocks + block_count]
    return result.reshape(block_count, 2 * reach_width - 1, tile_size * tile_size)
```

```python
import jax
import jax.numpy as jnp
from jax import lax
from jax.sharding import PartitionSpec as P


def metric_apply(metric, slab_rows):
    product = jnp.dot(
        metric, slab_rows.reshape(slab_rows.shape[0], -1), preferred_element_type=jnp.float32
    )
    return product.astype(jnp.bfloat16).reshape(slab_rows.shape)


def body(integrals, orbitals, locality, screen, metric):
    aux_rows, block_count, reach, tile, _ = integrals.shape
    n_aux = lax.axis_size("aux")
    first_block = lax.axis_index("bas") * block_count
    total_blocks = block_count * lax.axis_size("bas")
    chosen = jnp.take(integrals, locality, axis=1)
    half_rows = lax.dot_general(
        chosen, orbitals, (((4,), (1,)), ((1,), (0,))), preferred_element_type=jnp.float32
    )
    offsets = jnp.arange(reach, dtype=jnp.int32)
    row_blocks = first_block + locality[:, None] + offsets[None, :] - 1
    inside = ((row_blocks >= 0) & (row_blocks < total_blocks)).astype(jnp.float32)
    keep_mask = screen[0].astype(jnp.float32) * inside
    half_rows = (half_rows * keep_mask[:, None, :, None, None]).astype(jnp.bfloat16)
    received = lax.all_to_all(half_rows, "aux", split_axis=0, concat_axis=1, tiled=True)
    fitted = metric_apply(metric, received[0])
    gram = lax.dot_general(
        fitted, fitted, (((0, 3), (0, 3)), ((), ())), preferred_element_type=jnp.float32
    )
    share = tile * tile // n_aux
    pieces = jnp.transpose(gram, (0, 2, 1, 3)).reshape(reach * reach, n_aux, share)
    pieces = jnp.transpose(pieces, (1, 0, 2))
    shares = lax.all_to_all(pieces, "aux", split_axis=0, concat_axis=0, tiled=True)
    ids = jnp.arange(block_count, dtype=jnp.int32)
    order = jnp.sum(jnp.where(locality[None, :] == ids[:, None], ids[None, :], 0), axis=1)
    by_block = jnp.take(shares, order, axis=0).reshape(block_count, reach, reach, share)
    padded = [
        jnp.pad(by_block[:, d], ((0, 0), (reach - 1 - d, d), (0, 0))) for d in range(reach)
    ]
    zero_row = jnp.zeros((1,) + padded[0].shape[1:], jnp.float32)
    from_below = lax.ppermute(padded[2][-1:], "bas", [(0, 1)])
    from_above = lax.ppermute(padded[0][:1], "bas", [(1, 0)])
    lower = jnp.concatenate([padded[0][1:], from_above], axis=0)
    upper = jnp.concatenate([from_below, padded[2][:-1]], axis=0)
    return lower + padded[1] + upper


def solution(mesh):
    placed = (
        P("aux", "bas", None, None, None),
        P("bas", None, None),
        P("bas"),
        P("aux", "bas", None),
        P(),
    )
    return jax.shard_map(
        body, mesh=mesh, in_specs=placed, out_specs=P("bas", None, "aux"), check_vma=False
    )
```

```python
import functools

import jax
import jax.numpy as jnp
from jax import lax
from jax.experimental import pallas as pl
from jax.experimental.pallas import tpu as pltpu
from jax.sharding import PartitionSpec as P

MESH = pl.DeviceIdType.MESH
GROUP = 16
CHUNKS = ((0, 32), (32, 32), (64, 32), (96, 16), (112, 16))


def partner(me, step):
    code = lax.rem(step * 27, 64)
    z = lax.rem(me // 16 + code // 16, 4)
    y = lax.rem(me // 4 + code // 4, 4)
    x = lax.rem(me + code, 4)
    return z * 16 + y * 4 + x


def exchange_kernel(
    ints_hbm, orbs_hbm, loc_ref, screen_ref, metric_ref, shares_ref,
    ints, orbs, send, recv, mixer, gram, pieces,
    load_sem, send_sem, recv_sem, out_send_sem, out_recv_sem, own_sem,
):
    me = lax.axis_index("aux")
    core = lax.axis_index("bas")
    n = lax.axis_size("aux")
    tile = orbs.shape[1]
    wide = send.shape[2]
    blocks = ints.shape[0]
    total_blocks = blocks * lax.axis_size("bas")

    load_ints = pltpu.make_async_copy(ints_hbm.at[0], ints, load_sem.at[0])
    load_orbs = pltpu.make_async_copy(orbs_hbm, orbs, load_sem.at[1])
    load_ints.start()
    load_orbs.start()

    barrier = pltpu.get_barrier_semaphore()

    @pl.loop(1, n)
    def _(step):
        pl.semaphore_signal(
            barrier, inc=1, device_id=(partner(me, step), core), device_id_type=MESH
        )

    load_ints.wait()
    load_orbs.wait()

    def half(target):
        block = loc_ref[target]
        rows = ints[block].reshape(wide, tile)
        product = lax.dot_general(
            orbs[target], rows, (((0,), (1,)), ((), ())), preferred_element_type=jnp.float32
        )
        parts = []
        for d in range(3):
            place = core * blocks + block + d - 1
            inside = (place >= 0) & (place < total_blocks)
            keep = jnp.where(inside, screen_ref[0, target, d], 0).astype(jnp.float32)
            parts.append(product[:, d * tile : (d + 1) * tile] * keep)
        return jnp.concatenate(parts, axis=1).astype(jnp.bfloat16)

    def row_copy(step, chunk):
        target = partner(me, step)
        first, count = CHUNKS[chunk]
        return pltpu.make_async_remote_copy(
            src_ref=send.at[target, pl.ds(first, count)],
            dst_ref=recv.at[me, pl.ds(first, count)],
            send_sem=send_sem,
            recv_sem=recv_sem.at[chunk],
            device_id=(target, core),
            device_id_type=MESH,
        )

    pl.semaphore_wait(barrier, n - 1)

    @pl.loop(1, n, unroll=3)
    def _(step):
        target = partner(me, step)
        send[target] = half(target)
        row_copy(step, 0).start()

    for chunk in range(1, len(CHUNKS)):

        @pl.loop(1, n)
        def _(step):
            row_copy(step, chunk).start()

    recv[me] = half(me)

    size = n * GROUP
    gram[...] = jnp.zeros_like(gram)
    spread = (
        lax.broadcasted_iota(jnp.int32, (n, size), 1) // GROUP
        == lax.broadcasted_iota(jnp.int32, (n, size), 0)
    ).astype(jnp.bfloat16)
    step_rows = 128

    @pl.loop(0, size // step_rows)
    def _(part):
        first = part * step_rows
        row = lax.broadcasted_iota(jnp.int32, (step_rows, n), 0) + first
        pick = (row // GROUP == lax.broadcasted_iota(jnp.int32, (step_rows, n), 1))
        rows = jnp.dot(
            pick.astype(jnp.bfloat16), metric_ref[...], preferred_element_type=jnp.float32
        ).astype(jnp.bfloat16)
        full = jnp.dot(rows, spread, preferred_element_type=jnp.float32)
        same = lax.rem(
            lax.broadcasted_iota(jnp.int32, (step_rows, size), 0) + first, GROUP
        ) == lax.rem(lax.broadcasted_iota(jnp.int32, (step_rows, size), 1), GROUP)
        mixer[pl.ds(pl.multiple_of(first, step_rows), step_rows)] = jnp.where(
            same, full, 0.0
        ).astype(jnp.bfloat16)

    for chunk, (first, count) in enumerate(CHUNKS):
        landed = recv.at[pl.ds(0, n - 1), pl.ds(first, count)]
        pltpu.make_async_copy(landed, landed, recv_sem.at[chunk]).wait()
        for start in range(first, first + count, GROUP):
            slab = recv[:, start : start + GROUP, :].reshape(size, wide)
            fitted = jnp.dot(
                mixer[...], slab, preferred_element_type=jnp.float32
            ).astype(jnp.bfloat16)
            gram[...] += lax.dot_general(
                fitted, fitted, (((0,), (0,)), ((), ())), preferred_element_type=jnp.float32
            )

    for d in range(3):
        pieces[:, d] = gram[d * tile : (d + 1) * tile, :].reshape(n, 2, wide)

    def share_copy(step):
        target = partner(me, step)
        return pltpu.make_async_remote_copy(
            src_ref=pieces.at[target],
            dst_ref=shares_ref.at[me],
            send_sem=out_send_sem,
            recv_sem=out_recv_sem,
            device_id=(target, core),
            device_id_type=MESH,
        )

    own = pltpu.make_async_copy(pieces.at[me], shares_ref.at[me], own_sem)
    own.start()

    @pl.loop(1, n)
    def _(step):
        share_copy(step).start()

    own.wait()
    sent = send.at[pl.ds(0, n - 1)]
    pltpu.make_async_copy(sent, sent, send_sem).wait()
    moved = pieces.at[pl.ds(0, n - 1)]
    pltpu.make_async_copy(moved, moved, out_recv_sem).wait()
    pltpu.make_async_copy(moved, moved, out_send_sem).wait()


def body(integrals, orbitals, locality, screen, metric):
    _, block_count, reach, tile, _ = integrals.shape
    n_aux = lax.axis_size("aux")
    wide = reach * tile
    size = n_aux * GROUP
    shares = pl.pallas_call(
        exchange_kernel,
        out_shape=jax.ShapeDtypeStruct((n_aux, reach, 2, wide), jnp.float32),
        in_specs=[
            pl.BlockSpec(memory_space=pl.ANY),
            pl.BlockSpec(memory_space=pl.ANY),
            pl.BlockSpec(memory_space=pltpu.SMEM),
            pl.BlockSpec(memory_space=pltpu.SMEM),
            pl.BlockSpec(memory_space=pltpu.VMEM),
        ],
        out_specs=pl.BlockSpec(memory_space=pl.ANY),
        scratch_shapes=[
            pltpu.VMEM((block_count, reach, tile, tile), jnp.bfloat16),
            pltpu.VMEM((n_aux, tile, tile), jnp.bfloat16),
            pltpu.VMEM((n_aux, tile, wide), jnp.bfloat16),
            pltpu.VMEM((n_aux, tile, wide), jnp.bfloat16),
            pltpu.VMEM((size, size), jnp.bfloat16),
            pltpu.VMEM((wide, wide), jnp.float32),
            pltpu.VMEM((n_aux, reach, 2, wide), jnp.float32),
            pltpu.SemaphoreType.DMA((2,)),
            pltpu.SemaphoreType.DMA,
            pltpu.SemaphoreType.DMA((len(CHUNKS),)),
            pltpu.SemaphoreType.DMA,
            pltpu.SemaphoreType.DMA,
            pltpu.SemaphoreType.DMA,
        ],
        compiler_params=pltpu.CompilerParams(
            collective_id=0, has_side_effects=True, vmem_limit_bytes=48 << 20
        ),
    )(integrals, orbitals, locality, screen, metric)
    ids = jnp.arange(block_count, dtype=jnp.int32)
    order = jnp.sum(jnp.where(locality[None, :] == ids[:, None], ids[None, :], 0), axis=1)
    by_block = jnp.take(shares, order, axis=0).reshape(block_count, reach, 2, reach, tile)
    by_block = jnp.transpose(by_block, (0, 1, 3, 2, 4)).reshape(block_count, reach, reach, -1)
    padded = [
        jnp.pad(by_block[:, d], ((0, 0), (reach - 1 - d, d), (0, 0))) for d in range(reach)
    ]
    from_below = lax.ppermute(padded[2][-1:], "bas", [(0, 1)])
    from_above = lax.ppermute(padded[0][:1], "bas", [(1, 0)])
    lower = jnp.concatenate([padded[0][1:], from_above], axis=0)
    upper = jnp.concatenate([from_below, padded[2][:-1]], axis=0)
    return lower + padded[1] + upper


def solution(mesh):
    placed = (
        P("aux", "bas", None, None, None),
        P("bas", None, None),
        P("bas"),
        P("aux", "bas", None),
        P(),
    )
    return jax.shard_map(
        body, mesh=mesh, in_specs=placed, out_specs=P("bas", None, "aux"), check_vma=False
    )
```

```python
import functools

import jax
import jax.numpy as jnp
from jax import lax
from jax.experimental import pallas as pl
from jax.experimental.pallas import tpu as pltpu
from jax.sharding import PartitionSpec as P

MESH = pl.DeviceIdType.MESH
GROUP = 16
CHUNKS = ((0, 32), (32, 32), (64, 32), (96, 16), (112, 16))


def partner(me, step):
    code = lax.rem(step * 27, 64)
    z = lax.rem(me // 16 + code // 16, 4)
    y = lax.rem(me // 4 + code // 4, 4)
    x = lax.rem(me + code, 4)
    return z * 16 + y * 4 + x


def exchange_kernel(
    ints_hbm, orbs_hbm, loc_hbm, screen_hbm, metric_hbm, band_ref,
    ints, orbs, loc_ref, screen_ref, order_ref, metric_ref, send, recv, mixer, gram, pieces,
    shares, rim, near, rows,
    load_sem, send_sem, recv_sem, out_send_sem, out_recv_sem, own_sem, rim_sem,
):
    me = lax.axis_index("aux")
    core = lax.axis_index("bas")
    n = lax.axis_size("aux")
    tile = orbs.shape[1]
    wide = send.shape[2]
    blocks = ints.shape[0]
    total_blocks = blocks * lax.axis_size("bas")

    loads = [
        pltpu.make_async_copy(source, target, load_sem.at[place])
        for place, (source, target) in enumerate(
            (
                (ints_hbm.at[0], ints),
                (orbs_hbm, orbs),
                (loc_hbm, loc_ref),
                (screen_hbm, screen_ref),
                (metric_hbm, metric_ref),
            )
        )
    ]
    for load in loads:
        load.start()

    barrier = pltpu.get_barrier_semaphore()
    pl.semaphore_signal(barrier, inc=1, device_id=(me, 1 - core), device_id_type=MESH)

    @pl.loop(1, n)
    def _(step):
        pl.semaphore_signal(
            barrier, inc=1, device_id=(partner(me, step), core), device_id_type=MESH
        )

    for load in loads:
        load.wait()

    def half(target):
        block = loc_ref[target]
        rows = ints[block].reshape(wide, tile)
        product = lax.dot_general(
            orbs[target], rows, (((0,), (1,)), ((), ())), preferred_element_type=jnp.float32
        )
        parts = []
        for d in range(3):
            place = core * blocks + block + d - 1
            inside = (place >= 0) & (place < total_blocks)
            keep = jnp.where(inside, screen_ref[d, 0, target], 0).astype(jnp.float32)
            parts.append(product[:, d * tile : (d + 1) * tile] * keep)
        return jnp.concatenate(parts, axis=1).astype(jnp.bfloat16)

    def row_copy(step, chunk):
        target = partner(me, step)
        first, count = CHUNKS[chunk]
        return pltpu.make_async_remote_copy(
            src_ref=send.at[target, pl.ds(first, count)],
            dst_ref=recv.at[me, pl.ds(first, count)],
            send_sem=send_sem,
            recv_sem=recv_sem.at[chunk],
            device_id=(target, core),
            device_id_type=MESH,
        )

    pl.semaphore_wait(barrier, n)

    @pl.loop(1, n, unroll=3)
    def _(step):
        target = partner(me, step)
        send[target] = half(target)
        row_copy(step, 0).start()

    for chunk in range(1, len(CHUNKS)):

        @pl.loop(1, n)
        def _(step):
            row_copy(step, chunk).start()

    recv[me] = half(me)

    @pl.loop(0, blocks)
    def _(block):
        def find(target, found):
            return jnp.where(loc_ref[target] == block, target, found)

        order_ref[block] = lax.fori_loop(0, blocks, find, jnp.int32(0), unroll=8)

    size = n * GROUP
    gram[...] = jnp.zeros_like(gram)
    spread = (
        lax.broadcasted_iota(jnp.int32, (n, size), 1) // GROUP
        == lax.broadcasted_iota(jnp.int32, (n, size), 0)
    ).astype(jnp.bfloat16)
    step_rows = 128

    @pl.loop(0, size // step_rows)
    def _(part):
        first = part * step_rows
        row = lax.broadcasted_iota(jnp.int32, (step_rows, n), 0) + first
        pick = (row // GROUP == lax.broadcasted_iota(jnp.int32, (step_rows, n), 1))
        rows = jnp.dot(
            pick.astype(jnp.bfloat16), metric_ref[...], preferred_element_type=jnp.float32
        ).astype(jnp.bfloat16)
        full = jnp.dot(rows, spread, preferred_element_type=jnp.float32)
        same = lax.rem(
            lax.broadcasted_iota(jnp.int32, (step_rows, size), 0) + first, GROUP
        ) == lax.rem(lax.broadcasted_iota(jnp.int32, (step_rows, size), 1), GROUP)
        mixer[pl.ds(pl.multiple_of(first, step_rows), step_rows)] = jnp.where(
            same, full, 0.0
        ).astype(jnp.bfloat16)

    for chunk, (first, count) in enumerate(CHUNKS):
        landed = recv.at[pl.ds(0, n - 1), pl.ds(first, count)]
        pltpu.make_async_copy(landed, landed, recv_sem.at[chunk]).wait()
        for start in range(first, first + count, GROUP):
            slab = recv[:, start : start + GROUP, :].reshape(size, wide)
            fitted = jnp.dot(
                mixer[...], slab, preferred_element_type=jnp.float32
            ).astype(jnp.bfloat16)
            gram[...] += lax.dot_general(
                fitted, fitted, (((0,), (0,)), ((), ())), preferred_element_type=jnp.float32
            )

    for d in range(3):
        pieces[:, d] = gram[d * tile : (d + 1) * tile, :].reshape(n, 2, wide)

    def share_copy(step):
        target = partner(me, step)
        return pltpu.make_async_remote_copy(
            src_ref=pieces.at[target],
            dst_ref=shares.at[me],
            send_sem=out_send_sem,
            recv_sem=out_recv_sem,
            device_id=(target, core),
            device_id_type=MESH,
        )

    @pl.loop(1, n)
    def _(step):
        share_copy(step).start()

    own = pltpu.make_async_copy(pieces.at[me], shares.at[me], own_sem)
    own.start()
    sent = send.at[pl.ds(0, n - 1)]
    pltpu.make_async_copy(sent, sent, send_sem).wait()
    own.wait()
    moved = pieces.at[pl.ds(0, n - 1)]
    pltpu.make_async_copy(moved, moved, out_recv_sem).wait()
    edge = jnp.where(core == 0, blocks - 1, 0)
    rim[...] = shares[order_ref[edge], 2 * (1 - core)]
    rim_copy = pltpu.make_async_remote_copy(
        src_ref=rim,
        dst_ref=near,
        send_sem=rim_sem.at[0],
        recv_sem=rim_sem.at[1],
        device_id=(me, 1 - core),
        device_id_type=MESH,
    )
    rim_copy.start()

    def put(place, pieces_of_d):
        for e in range(5):
            terms = [
                piece[:, (e - 2 + d) * tile : (e - 1 + d) * tile]
                for d, piece in enumerate(pieces_of_d)
                if 0 <= e - 2 + d < 3
            ]
            rows[e, place] = functools.reduce(lambda left, right: left + right, terms)

    @pl.loop(1, blocks - 1, unroll=2)
    def _(place):
        put(place, [shares[order_ref[place + 1 - d], d] for d in range(3)])

    def lay(first, count):
        for e in range(5):
            for b in range(2):
                band_ref[e, first : first + count, b * tile : (b + 1) * tile] = rows[
                    e, first : first + count, b
                ]

    lay(8, blocks - 16)
    pltpu.make_async_copy(moved, moved, out_send_sem).wait()
    rim_copy.wait()
    other = near[...]
    none = jnp.zeros_like(other)
    first_rows = [shares[order_ref[1 - d], d] for d in range(2)]
    put(0, first_rows + [jnp.where(core == 0, none, other)])
    last_rows = [shares[order_ref[blocks - d], d] for d in range(1, 3)]
    put(blocks - 1, [jnp.where(core == 0, other, none)] + last_rows)
    lay(0, 8)
    lay(blocks - 8, 8)


def body(integrals, orbitals, locality, screen, metric):
    _, block_count, reach, tile, _ = integrals.shape
    n_aux = lax.axis_size("aux")
    wide = reach * tile
    size = n_aux * GROUP
    hbm = pl.BlockSpec(memory_space=pltpu.HBM)
    band = pl.pallas_call(
        exchange_kernel,
        out_shape=jax.ShapeDtypeStruct((2 * reach - 1, block_count, 2 * tile), jnp.float32),
        in_specs=[hbm] * 5,
        out_specs=pl.BlockSpec(memory_space=pltpu.VMEM),
        scratch_shapes=[
            pltpu.VMEM((block_count, reach, tile, tile), jnp.bfloat16),
            pltpu.VMEM((n_aux, tile, tile), jnp.bfloat16),
            pltpu.SMEM((block_count,), jnp.int32),
            pltpu.SMEM((reach, 1, n_aux), jnp.int32),
            pltpu.SMEM((block_count,), jnp.int32),
            pltpu.VMEM((n_aux, n_aux), jnp.bfloat16),
            pltpu.VMEM((n_aux, tile, wide), jnp.bfloat16),
            pltpu.VMEM((n_aux, tile, wide), jnp.bfloat16),
            pltpu.VMEM((size, size), jnp.bfloat16),
            pltpu.VMEM((wide, wide), jnp.float32),
            pltpu.VMEM((n_aux, reach, 2, wide), jnp.float32),
            pltpu.VMEM((n_aux, reach, 2, wide), jnp.float32),
            pltpu.VMEM((2, wide), jnp.float32),
            pltpu.VMEM((2, wide), jnp.float32),
            pltpu.VMEM((2 * reach - 1, block_count, 2, tile), jnp.float32),
            pltpu.SemaphoreType.DMA((5,)),
            pltpu.SemaphoreType.DMA,
            pltpu.SemaphoreType.DMA((len(CHUNKS),)),
            pltpu.SemaphoreType.DMA,
            pltpu.SemaphoreType.DMA,
            pltpu.SemaphoreType.DMA,
            pltpu.SemaphoreType.DMA((2,)),
        ],
        compiler_params=pltpu.CompilerParams(
            collective_id=0, has_side_effects=True, vmem_limit_bytes=63 << 20
        ),
    )(integrals, orbitals, locality, jnp.transpose(screen, (2, 0, 1)), metric)
    return jnp.transpose(band, (1, 0, 2))


def solution(mesh):
    placed = (
        P("aux", "bas", None, None, None),
        P("bas", None, None),
        P("bas"),
        P("aux", "bas", None),
        P(),
    )
    return jax.shard_map(
        body, mesh=mesh, in_specs=placed, out_specs=P("bas", None, "aux"), check_vma=False
    )
```

```python
import functools

import jax
import jax.numpy as jnp
from jax import lax
from jax.experimental import pallas as pl
from jax.experimental.pallas import tpu as pltpu
from jax.sharding import PartitionSpec as P

MESH = pl.DeviceIdType.MESH
GROUP = 16
CHUNKS = ((0, 32), (32, 32), (64, 32), (96, 16), (112, 16))


def partner(me, step):
    code = lax.rem(step * 27, 64)
    z = lax.rem(me // 16 + code // 16, 4)
    y = lax.rem(me // 4 + code // 4, 4)
    x = lax.rem(me + code, 4)
    return z * 16 + y * 4 + x


def exchange_kernel(
    ints_hbm, orbs_hbm, loc_hbm, screen_hbm, metric_hbm, band_ref,
    ints, orbs, loc_ref, screen_ref, order_ref, metric_ref, send, recv, mixer, gram, shares,
    load_sem, send_sem, recv_sem, out_send_sem, out_recv_sem, own_sem, rim_sem,
):
    me = lax.axis_index("aux")
    core = lax.axis_index("bas")
    n = lax.axis_size("aux")
    tile = orbs.shape[1]
    wide = send.shape[2]
    blocks = ints.shape[0]
    total_blocks = blocks * lax.axis_size("bas")
    edge = jnp.where(core == 0, blocks - 1, 0)
    other_edge = jnp.where(core == 0, 0, blocks - 1)

    loads = [
        pltpu.make_async_copy(source, target, load_sem.at[place])
        for place, (source, target) in enumerate(
            (
                (loc_hbm, loc_ref),
                (ints_hbm.at[0], ints),
                (orbs_hbm, orbs),
                (screen_hbm, screen_ref),
                (metric_hbm, metric_ref),
            )
        )
    ]
    for load in loads:
        load.start()

    barrier = pltpu.get_barrier_semaphore()

    @pl.loop(1, n)
    def _(step):
        pl.semaphore_signal(
            barrier, inc=1, device_id=(partner(me, step), core), device_id_type=MESH
        )

    pl.semaphore_signal(
        barrier, inc=1, device_id=(other_edge, 1 - core), device_id_type=MESH
    )
    loads[0].wait()

    @pl.loop(0, blocks)
    def _(block):
        found = jnp.int32(0)
        for index in range(blocks):
            found = jnp.where(loc_ref[index] == block, index, found)
        order_ref[block] = found

    for load in loads[1:]:
        load.wait()

    def half(block):
        index = order_ref[block]
        rows = ints[block].reshape(wide, tile)
        product = lax.dot_general(
            orbs[index], rows, (((0,), (1,)), ((), ())), preferred_element_type=jnp.float32
        )
        parts = []
        for d in range(3):
            place = core * blocks + block + d - 1
            inside = (place >= 0) & (place < total_blocks)
            keep = jnp.where(inside, screen_ref[d, 0, index], 0).astype(jnp.float32)
            parts.append(product[:, d * tile : (d + 1) * tile] * keep)
        return jnp.concatenate(parts, axis=1).astype(jnp.bfloat16)

    def row_copy(step, chunk):
        target = partner(me, step)
        first, count = CHUNKS[chunk]
        return pltpu.make_async_remote_copy(
            src_ref=send.at[target, pl.ds(first, count)],
            dst_ref=recv.at[me, pl.ds(first, count)],
            send_sem=send_sem,
            recv_sem=recv_sem.at[chunk],
            device_id=(target, core),
            device_id_type=MESH,
        )

    pl.semaphore_wait(barrier, jnp.where(me == edge, 2 * n - 1, n - 1))

    @pl.loop(1, n, unroll=3)
    def _(step):
        target = partner(me, step)
        send[target] = half(target)
        row_copy(step, 0).start()

    for chunk in range(1, len(CHUNKS)):

        @pl.loop(1, n)
        def _(step):
            row_copy(step, chunk).start()

    recv[me] = half(me)

    size = n * GROUP
    gram[...] = jnp.zeros_like(gram)
    spread = (
        lax.broadcasted_iota(jnp.int32, (n, size), 1) // GROUP
        == lax.broadcasted_iota(jnp.int32, (n, size), 0)
    ).astype(jnp.bfloat16)
    step_rows = 128

    @pl.loop(0, size // step_rows)
    def _(part):
        first = part * step_rows
        row = lax.broadcasted_iota(jnp.int32, (step_rows, n), 0) + first
        pick = (row // GROUP == lax.broadcasted_iota(jnp.int32, (step_rows, n), 1))
        rows = jnp.dot(
            pick.astype(jnp.bfloat16), metric_ref[...], preferred_element_type=jnp.float32
        ).astype(jnp.bfloat16)
        full = jnp.dot(rows, spread, preferred_element_type=jnp.float32)
        same = lax.rem(
            lax.broadcasted_iota(jnp.int32, (step_rows, size), 0) + first, GROUP
        ) == lax.rem(lax.broadcasted_iota(jnp.int32, (step_rows, size), 1), GROUP)
        mixer[pl.ds(pl.multiple_of(first, step_rows), step_rows)] = jnp.where(
            same, full, 0.0
        ).astype(jnp.bfloat16)

    for chunk, (first, count) in enumerate(CHUNKS):
        landed = recv.at[pl.ds(0, n - 1), pl.ds(first, count)]
        pltpu.make_async_copy(landed, landed, recv_sem.at[chunk]).wait()
        for start in range(first, first + count, GROUP):
            slab = recv[:, start : start + GROUP, :].reshape(size, wide)
            fitted = jnp.dot(
                mixer[...], slab, preferred_element_type=jnp.float32
            ).astype(jnp.bfloat16)
            product = lax.dot_general(
                fitted, fitted, (((0,), (0,)), ((), ())), preferred_element_type=jnp.float32
            )
            for d in range(3):
                for d2 in range(3):
                    gram[3 * d + d2] += product[
                        d * tile : (d + 1) * tile, d2 * tile : (d2 + 1) * tile
                    ]

    pieces = gram.reshape(9, n, 2, tile)
    top = blocks + 8

    def share_copy(step):
        target = partner(me, step)
        return pltpu.make_async_remote_copy(
            src_ref=pieces.at[:, target],
            dst_ref=shares.at[:, :, me + 8, 0],
            send_sem=out_send_sem,
            recv_sem=out_recv_sem,
            device_id=(target, core),
            device_id_type=MESH,
        )

    def rim_copy(target):
        return pltpu.make_async_remote_copy(
            src_ref=pieces.at[pl.ds(6 * (1 - core), 3), target],
            dst_ref=shares.at[pl.ds(6 * (1 - core), 3), :, jnp.where(core == 0, 7, top), 0],
            send_sem=rim_sem.at[0],
            recv_sem=rim_sem.at[1],
            device_id=(target, 1 - core),
            device_id_type=MESH,
        )

    @pl.when(me == edge)
    def _():
        @pl.loop(0, n)
        def _(target):
            rim_copy(target).start()

    @pl.loop(1, n)
    def _(step):
        share_copy(step).start()

    own = pltpu.make_async_copy(pieces.at[:, me], shares.at[:, :, me + 8, 0], own_sem)
    own.start()
    shares[pl.ds(6 * (1 - core), 3), :, jnp.where(core == 0, 7, top)] = jnp.zeros(
        (3, 2, 1, tile), jnp.float32
    )
    sent = send.at[pl.ds(0, n - 1)]
    pltpu.make_async_copy(sent, sent, send_sem).wait()
    own.wait()
    moved = pieces.at[:, pl.ds(0, n - 1)]
    pltpu.make_async_copy(moved, moved, out_recv_sem).wait()
    one = pieces.at[pl.ds(0, 3), 0]
    pltpu.make_async_copy(one, one, rim_sem.at[1]).wait()

    flat = shares.reshape(9, 2, blocks + 16, tile)
    for e in range(5):
        for b in range(2):
            terms = [
                flat[3 * d + e - 2 + d, b, 9 - d : 9 - d + blocks, :]
                for d in range(3)
                if 0 <= e - 2 + d < 3
            ]
            band_ref[e, :, b * tile : (b + 1) * tile] = functools.reduce(
                lambda left, right: left + right, terms
            )

    pltpu.make_async_copy(moved, moved, out_send_sem).wait()

    @pl.when(me == edge)
    def _():
        every = pieces.at[pl.ds(0, 3)]
        pltpu.make_async_copy(every, every, rim_sem.at[0]).wait()


def body(integrals, orbitals, locality, screen, metric):
    _, block_count, reach, tile, _ = integrals.shape
    n_aux = lax.axis_size("aux")
    wide = reach * tile
    size = n_aux * GROUP
    hbm = pl.BlockSpec(memory_space=pltpu.HBM)
    band = pl.pallas_call(
        exchange_kernel,
        out_shape=jax.ShapeDtypeStruct((2 * reach - 1, block_count, 2 * tile), jnp.float32),
        in_specs=[hbm] * 5,
        out_specs=pl.BlockSpec(memory_space=pltpu.VMEM),
        scratch_shapes=[
            pltpu.VMEM((block_count, reach, tile, tile), jnp.bfloat16),
            pltpu.VMEM((n_aux, tile, tile), jnp.bfloat16),
            pltpu.SMEM((block_count,), jnp.int32),
            pltpu.SMEM((reach, 1, n_aux), jnp.int32),
            pltpu.SMEM((block_count,), jnp.int32),
            pltpu.VMEM((n_aux, n_aux), jnp.bfloat16),
            pltpu.VMEM((n_aux, tile, wide), jnp.bfloat16),
            pltpu.VMEM((n_aux, tile, wide), jnp.bfloat16),
            pltpu.VMEM((size, size), jnp.bfloat16),
            pltpu.VMEM((reach * reach, tile, tile), jnp.float32),
            pltpu.VMEM((reach * reach, 2, block_count + 16, 1, tile), jnp.float32),
            pltpu.SemaphoreType.DMA((5,)),
            pltpu.SemaphoreType.DMA,
            pltpu.SemaphoreType.DMA((len(CHUNKS),)),
            pltpu.SemaphoreType.DMA,
            pltpu.SemaphoreType.DMA,
            pltpu.SemaphoreType.DMA,
            pltpu.SemaphoreType.DMA((2,)),
        ],
        compiler_params=pltpu.CompilerParams(
            collective_id=0, has_side_effects=True, vmem_limit_bytes=63 << 20
        ),
    )(integrals, orbitals, locality, jnp.transpose(screen, (2, 0, 1)), metric)
    return jnp.transpose(band, (1, 0, 2))


def solution(mesh):
    placed = (
        P("aux", "bas", None, None, None),
        P("bas", None, None),
        P("bas"),
        P("aux", "bas", None),
        P(),
    )
    return jax.shard_map(
        body, mesh=mesh, in_specs=placed, out_specs=P("bas", None, "aux"), check_vma=False
    )
```
